32 devices in a mesh: gx: 4 (over y, core), gy: 8 (over z, x).
Axes of the slice: x: 2, y: 2, z: 4, core: 2. Of those that a mesh axis runs over, the one named last changes fastest.
Arguments:
- hidden_in: bfloat16 [3072, 2304], P('gy', 'gx'), may hold values from -6 to 6
- out_grad: bfloat16 [3072, 2304], P('gy', 'gx'), may hold values from -6 to 6
- seq_ids: int32 [3072], replicated, may hold values from 0 to 2, never falling along the last dimension, each value on 1 to 2048 neighbouring positions
- qkv_weight: bfloat16 [2304, 4, 1024], P('gy', 'gx'), may hold values from -0.25 to 0.25
- out_weight: bfloat16 [2048, 2304], P('gx', 'gy'), may hold values from -0.75 to 0.75
- gate_up_weight: bfloat16 [2304, 2, 9216], P('gy', None, 'gx'), may hold values from -0.125 to 0.125
- down_weight: bfloat16 [9216, 2304], P('gx', 'gy'), may hold values from -0.0625 to 0.0625
- norm_gains: bfloat16 [4, 2304], P(None, 'gy'), may hold values from -0.59765625 to 0.59765625
- moment_qkv: float32 [2304, 4, 1024], P('gy', 'gx'), may hold values from -112 to 112
- moment_out: float32 [2048, 2304], P('gx', 'gy'), may hold values from -10 to 10
- moment_gate_up: float32 [2304, 2, 9216], P('gy', None, 'gx'), may hold values from -16 to 16
- moment_down: float32 [9216, 2304], P('gx', 'gy'), may hold values from -32 to 32
- moment_gains: float32 [4, 2304], P(None, 'gy'), may hold values from -56 to 56
- square_qkv: float32 [2304, 4, 1024], P('gy', 'gx'), may hold values from 768 to 3072
- square_out: float32 [2048, 2304], P('gx', 'gy'), may hold values from 7.68 to 30.72
- square_gate_up: float32 [2304, 2, 9216], P('gy', None, 'gx'), may hold values from 21.504 to 82.944
- square_down: float32 [9216, 2304], P('gx', 'gy'), may hold values from 82.944 to 307.2
- square_gains: float32 [4, 2304], P(None, 'gy'), may hold values from 184.32 to 737.28
Outputs:
- block_out: bfloat16 [3072, 2304], P('gy', 'gx')
- input_grad: float32 [3072, 2304], P('gy', 'gx')
- grad_qkv: float32 [2304, 4, 1024], P('gy', 'gx')
- grad_out: float32 [2048, 2304], P('gx', 'gy')
- grad_gate_up: float32 [2304, 2, 9216], P('gy', None, 'gx')
- grad_down: float32 [9216, 2304], P('gx', 'gy')
- grad_gains: float32 [4, 2304], P(None, 'gy')
- moment_qkv_new: float32 [2304, 4, 1024], P('gy', 'gx')
- moment_out_new: float32 [2048, 2304], P('gx', 'gy')
- moment_gate_up_new: float32 [2304, 2, 9216], P('gy', None, 'gx')
- moment_down_new: float32 [9216, 2304], P('gx', 'gy')
- moment_gains_new: float32 [4, 2304], P(None, 'gy')
- square_qkv_new: float32 [2304, 4, 1024], P('gy', 'gx')
- square_out_new: float32 [2048, 2304], P('gx', 'gy')
- square_gate_up_new: float32 [2304, 2, 9216], P('gy', None, 'gx')
- square_down_new: float32 [9216, 2304], P('gx', 'gy')
- square_gains_new: float32 [4, 2304], P(None, 'gy')
- update_qkv: float32 [2304, 4, 1024], P('gy', 'gx')
- update_out: float32 [2048, 2304], P('gx', 'gy')
- update_gate_up: float32 [2304, 2, 9216], P('gy', None, 'gx')
- update_down: float32 [9216, 2304], P('gx', 'gy')
- update_gains: float32 [4, 2304], P(None, 'gy')
The draws below stay inside these ranges and needn't reach their ends.
Inputs may be any that keep to these rules, and one draw needn't show every extreme that they name: `seq_ids`: sequence numbers never fall along the tokens; every sequence has 1 to 2048 tokens, and one has exactly 2048.
All inputs are finite; a program needn't handle non-finite values.
Results may differ from the reference program's by a relative error of at most 0.03.
The reference program's roundings to bfloat16 on the way count: a program that leaves them out, or rounds other values in their place, can miss the bound.
Values may be sent and summed in bfloat16 or wider, within the bound.
No kernel may reach another device: no remote copies, remote signals or barrier semaphores. Data moves between devices by JAX's collectives and lax.ppermute only.
A program may use at most 320 MiB of HBM per device.

```python
import math
import jax
import jax.numpy as jnp
import numpy as np
from jax import lax

D = 2304
FF = 9216
HEADS = 8
KV = 4
HEAD = 256
TOK_DEV = 384
TOKENS = 3072
SEQS = 3
MOST_LEN = 2048
REACH = 6


def draw_qkv_weight(key, part):
    col_count = (HEADS // KV + 2) * HEAD
    drawn_draw = jax.random.truncated_normal(key, -4.0, 4.0, (D, KV, col_count), jnp.float32)
    chosen = jax.random.randint(jax.random.fold_in(key, 7), (), 0, KV)
    head_pick = (jnp.arange(KV) == chosen)[None, :, None]
    column_pick = (jnp.arange(col_count) < (HEADS // KV + 1) * HEAD)[None, None, :]
    boost_factor = jnp.where(head_pick & column_pick, 3.0, 1.0)
    return (drawn_draw * boost_factor * D ** (-0.5)).astype(jnp.bfloat16)


def steps_of(own_key, dims, shards, least, high):
    def one(position, parts):
        draws = jax.random.uniform(jax.random.fold_in(jax.random.fold_in(own_key, 6), position), (parts,), jnp.float32, least / len(shards), high / len(shards))
        return jnp.repeat(jnp.exp(draws), dims[position] // parts).reshape((-1,) + (1,) * (len(dims) - position - 1))

    gain = one(*shards[0])
    for cut in shards[1:]:
        gain = gain * one(*cut)
    return gain


def split_up(count, total, reach, slope):
    weights = [(1 << 20) // math.isqrt(rank ** slope) + 1 for rank in range(2, count + 1)]
    surplus, given = total - reach - (count - 1), [1] * (count - 1)
    while surplus > 0:
        free = [i for i in range(count - 1) if given[i] < reach]
        mass, budget = sum([weights[i] for i in free]), surplus
        for i in free:
            extra = min(reach - given[i], max(1, budget * weights[i] // mass), surplus)
            given[i] = given[i] + extra
            surplus = surplus - extra
    return np.array([reach] + given)


def ragged_sizes(rng, amount, total, bound, skew):
    if amount == 2:
        one = jax.random.randint(rng, (), max(1, total - bound), min(bound, total - 1) + 1)
        return jnp.stack([one, total - one])
    sizes = jnp.asarray(split_up(amount, total, bound, skew), jnp.int32)
    couples = (amount - 1) // 2
    source_of, sink = sizes[1:1 + 2 * couples:2], sizes[2:2 + 2 * couples:2]
    slack = jnp.minimum(source_of - 1, bound - sink)
    shifted = jax.random.randint(jax.random.fold_in(rng, 1), (couples,), 0, 1 << 20) % (slack + 1)
    sizes = sizes.at[1:1 + 2 * couples:2].set(source_of - shifted).at[2:2 + 2 * couples:2].set(sink + shifted)
    return sizes[jax.random.permutation(jax.random.fold_in(rng, 2), amount)]


def noise(stream_key, dims, spread, limit, shards=(), held_as=jnp.bfloat16):
    loudness = steps_of(stream_key, dims, shards, -0.22, 0.18) if shards else 1.0
    values = jax.random.normal(stream_key, dims, jnp.float32) * spread * loudness
    return jnp.minimum(jnp.maximum(values, -limit), limit).astype(held_as)


def setup_inputs(seed: int = 0) -> dict:
    splits = jax.random.split(jax.random.key(seed), 19)
    hidden_in = noise(splits[0], (TOKENS, D), 1.0, 6.0, ((0, 8), (1, 4)))
    out_grad = noise(splits[1], (TOKENS, D), 1.0, 6.0, ((0, 8), (1, 4)))
    seq_ids = jnp.searchsorted(jnp.cumsum(ragged_sizes(splits[2], SEQS, TOKENS, MOST_LEN, 1)), jnp.arange(TOKENS), side="right").astype(jnp.int32)
    qkv_weight = draw_qkv_weight(jax.random.fold_in(splits[18], 71), 0)
    out_weight = noise(splits[4], (HEADS * HEAD, D), (HEADS * HEAD // 32) ** -0.5, 0.75, ((0, 4), (1, 8)))
    gate_up_weight = noise(splits[5], (D, 2, FF), D ** -0.5, 0.125, ((0, 8), (2, 4)))
    down_weight = noise(splits[6], (FF, D), FF ** -0.5, 0.0625, ((0, 4), (1, 8)))
    norm_gains = noise(splits[7], (4, D), 0.15, 0.59765625, ((1, 8),))
    moment_qkv = noise(splits[8], (D, KV, (HEADS // KV + 2) * HEAD), (0.33 * TOKENS ** 0.5), 112.0, ((0, 8), (1, 4)), jnp.float32)
    moment_out = noise(splits[9], (HEADS * HEAD, D), (0.033 * TOKENS ** 0.5), 10.0, ((0, 4), (1, 8)), jnp.float32)
    moment_gate_up = noise(splits[10], (D, 2, FF), (0.055 * TOKENS ** 0.5), 16.0, ((0, 8), (2, 4)), jnp.float32)
    moment_down = noise(splits[11], (FF, D), (0.11 * TOKENS ** 0.5), 32.0, ((0, 4), (1, 8)), jnp.float32)
    moment_gains = noise(splits[12], (4, D), (0.165 * TOKENS ** 0.5), 56.0, ((1, 8),), jnp.float32)
    square_qkv = jnp.clip(jnp.exp(math.log(3072.0) - 1.3862944 * jax.random.uniform(splits[13], (D, KV, (HEADS // KV + 2) * HEAD), jnp.float32) ** steps_of(splits[13], (D, KV, (HEADS // KV + 2) * HEAD), ((0, 8), (1, 4)), -0.2, 0.2)), 768.0, 3072.0)
    square_out = jnp.clip(jnp.exp(math.log(30.72) - 1.3862944 * jax.random.uniform(splits[14], (HEADS * HEAD, D), jnp.float32) ** steps_of(splits[14], (HEADS * HEAD, D), ((0, 4), (1, 8)), -0.2, 0.2)), 7.68, 30.72)
    square_gate_up = jnp.clip(jnp.exp(math.log(82.944) - 1.3499267 * jax.random.uniform(splits[15], (D, 2, FF), jnp.float32) ** steps_of(splits[15], (D, 2, FF), ((0, 8), (2, 4)), -0.2, 0.2)), 21.504, 82.944)
    square_down = jnp.clip(jnp.exp(math.log(307.2) - 1.30933336 * jax.random.uniform(splits[16], (FF, D), jnp.float32) ** steps_of(splits[16], (FF, D), ((0, 4), (1, 8)), -0.2, 0.2)), 82.944, 307.2)
    square_gains = jnp.clip(jnp.exp(math.log(737.28) - 1.3862944 * jax.random.uniform(splits[17], (4, D), jnp.float32) ** steps_of(splits[17], (4, D), ((1, 8),), -0.2, 0.2)), 184.32, 737.28)
    return {"hidden_in": hidden_in, "out_grad": out_grad, "seq_ids": seq_ids, "qkv_weight": qkv_weight, "out_weight": out_weight, "gate_up_weight": gate_up_weight, "down_weight": down_weight, "norm_gains": norm_gains, "moment_qkv": moment_qkv, "moment_out": moment_out, "moment_gate_up": moment_gate_up, "moment_down": moment_down, "moment_gains": moment_gains, "square_qkv": square_qkv, "square_out": square_out, "square_gate_up": square_gate_up, "square_down": square_down, "square_gains": square_gains}


NORM_EPS = 1e-06
SOFT_CAP = 50.0
MASKED_SCORE = -1e+30
BETA_ONE = 0.9
BETA_TWO = 0.95
FIRST_FIX = 1.0 - 0.9 ** 10
SECOND_FIX = 1.0 - 0.95 ** 10
LEARN_RATE = 0.05
WEIGHT_DECAY = 0.1
ADAM_EPS = 1e-08

@jax.custom_vjp
def low(v):
    return lax.optimization_barrier(v.astype(jnp.bfloat16)).astype(jnp.float32)

@jax.custom_vjp
def low_back(v):
    return v

def low_keep(v):
    return (low(v), None)

def low_pass(kept, grad):
    return (grad,)

def back_keep(v):
    return (v, None)

def back_low(kept, grad):
    return (low(grad),)
low.defvjp(low_keep, low_pass)
low_back.defvjp(back_keep, back_low)

def rms_norm(values, gain_row):
    return values * lax.rsqrt(lax.optimization_barrier(jnp.mean(values * values, axis=-1, keepdims=True)) + NORM_EPS) * (1.0 + gain_row)

def rotate(tensor, cosine, sine_part):
    half_dim = tensor.shape[-1] // 2
    leading = tensor[..., :half_dim]
    trailing = tensor[..., half_dim:]
    return jnp.concatenate([leading * cosine - trailing * sine_part, trailing * cosine + leading * sine_part], axis=-1)

def adamw_step(weight, gradient, moment, square):
    weight_wide = weight.astype(jnp.float32)
    moment_new = BETA_ONE * moment + (1.0 - BETA_ONE) * gradient
    square_new = BETA_TWO * square + (1.0 - BETA_TWO) * gradient * gradient
    update = -LEARN_RATE * (moment_new / FIRST_FIX / (jnp.sqrt(square_new / SECOND_FIX) + ADAM_EPS) + WEIGHT_DECAY * weight_wide)
    return (moment_new, square_new, update)

def rowwise(function, arrays):
    blocks = TOKENS // TOK_DEV
    shaped = jax.tree.map(lambda member: member.reshape((blocks, TOK_DEV) + member.shape[1:]), arrays)
    result = lax.map(jax.checkpoint(function), shaped)
    return jax.tree.map(lambda member: member.reshape((TOKENS,) + member.shape[2:]), result)

def attention(query_rot, key_rot, value_low, seq_ids):
    pad_rows = REACH * TOK_DEV
    window = (REACH + 1) * TOK_DEV
    keys_pad = jnp.concatenate([jnp.zeros((pad_rows,) + key_rot.shape[1:], key_rot.dtype), key_rot], axis=0)
    values_pad = jnp.concatenate([jnp.zeros((pad_rows,) + value_low.shape[1:], value_low.dtype), value_low], axis=0)
    seq_pad = jnp.concatenate([jnp.full((pad_rows,), -1, jnp.int32), seq_ids.astype(jnp.int32)], axis=0)

    def one_block(block_index):
        begin_row = (block_index * TOK_DEV).astype(jnp.int32)
        query_blk = lax.dynamic_slice_in_dim(query_rot, begin_row, TOK_DEV, 0)
        key_blk = lax.dynamic_slice_in_dim(keys_pad, begin_row, window, 0)
        value_blk = lax.dynamic_slice_in_dim(values_pad, begin_row, window, 0)
        query_seq = lax.dynamic_slice_in_dim(seq_ids.astype(jnp.int32), begin_row, TOK_DEV, 0)
        key_seq = lax.dynamic_slice_in_dim(seq_pad, begin_row, window, 0)
        query_pos = begin_row + jnp.arange(TOK_DEV, dtype=jnp.int32)
        key_pos = begin_row - pad_rows + jnp.arange(window, dtype=jnp.int32)
        allowed = (key_seq[None, :] == query_seq[:, None]) & (key_pos[None, :] <= query_pos[:, None])
        raw_scores = low_back(jnp.einsum('qkgd,skd->kgqs', query_blk, key_blk, precision=lax.Precision.HIGHEST))
        capped = SOFT_CAP * jnp.tanh(raw_scores / SOFT_CAP)
        scores = jnp.where(allowed[None, None], capped, MASKED_SCORE)
        row_top = lax.optimization_barrier(jnp.max(scores, axis=-1, keepdims=True))
        exp_scores = jnp.exp(scores - row_top)
        attn_probs = exp_scores / lax.optimization_barrier(jnp.sum(exp_scores, axis=-1, keepdims=True))
        return jnp.einsum('kgqs,skd->qkgd', low(attn_probs), value_blk, precision=lax.Precision.HIGHEST)
    blocks = TOKENS // TOK_DEV
    result = lax.map(jax.checkpoint(one_block), jnp.arange(blocks, dtype=jnp.int32))
    return result.reshape((TOKENS,) + result.shape[2:])

def forward(hidden, qkv_wide, out_wide, gate_up_wide, down_wide, gains_wide, seq_ids):
    group_size = HEADS // KV
    inverse = jnp.exp(jnp.arange(HEAD // 2, dtype=jnp.float32) * (-2.0 * math.log(10000.0) / HEAD))
    positions = jnp.arange(TOKENS, dtype=jnp.int32).astype(jnp.float32)

    def front_half(pieces):
        rows_in, rows_pos = pieces
        row_count = rows_in.shape[0]
        angles = rows_pos[:, None] * inverse[None, :]
        cosine = jnp.cos(angles)
        sine_part = jnp.sin(angles)
        normed = low(rms_norm(rows_in, gains_wide[0]))
        projected = low_back(jnp.einsum('td,dkc->tkc', normed, qkv_wide, precision=lax.Precision.HIGHEST))
        query_raw = projected[:, :, :group_size * HEAD].reshape(row_count, KV, group_size, HEAD)
        key_raw = projected[:, :, group_size * HEAD:(group_size + 1) * HEAD]
        value_raw = projected[:, :, (group_size + 1) * HEAD:]
        query_rot = low(rotate(query_raw, cosine[:, None, None, :], sine_part[:, None, None, :]) * HEAD ** (-0.5))
        key_rot = low(rotate(key_raw, cosine[:, None, :], sine_part[:, None, :]))
        return (query_rot, key_rot, low(value_raw))

    def back_half(pieces):
        rows_in, rows_attn = pieces
        mixed_sum = low_back(jnp.dot(rows_attn, out_wide, precision=lax.Precision.HIGHEST))
        resid_sum = rows_in + rms_norm(mixed_sum, gains_wide[1])
        normed = low(rms_norm(resid_sum, gains_wide[2]))
        gate_up_val = low_back(jnp.einsum('td,dcf->tcf', normed, gate_up_wide, precision=lax.Precision.HIGHEST))
        hidden_act = low(jax.nn.gelu(gate_up_val[:, 0], approximate=True) * gate_up_val[:, 1])
        down_sum = low_back(jnp.dot(hidden_act, down_wide, precision=lax.Precision.HIGHEST))
        return resid_sum + rms_norm(down_sum, gains_wide[3])
    query_rot, key_rot, value_low = rowwise(front_half, (hidden, positions))
    attended = attention(query_rot, key_rot, value_low, seq_ids)
    attn_low = low_back(low(attended)).reshape(TOKENS, HEADS * HEAD)
    return rowwise(back_half, (hidden, attn_low))

def reference(hidden_in, out_grad, seq_ids, qkv_weight, out_weight, gate_up_weight, down_weight, norm_gains, moment_qkv, moment_out, moment_gate_up, moment_down, moment_gains, square_qkv, square_out, square_gate_up, square_down, square_gains):

    def whole_block(hidden, qkv_wide, out_wide, gate_up_wide, down_wide, gains_wide):
        return forward(hidden, qkv_wide, out_wide, gate_up_wide, down_wide, gains_wide, seq_ids)
    block_val, pull_back = jax.vjp(whole_block, hidden_in.astype(jnp.float32), qkv_weight.astype(jnp.float32), out_weight.astype(jnp.float32), gate_up_weight.astype(jnp.float32), down_weight.astype(jnp.float32), norm_gains.astype(jnp.float32))
    input_grad, grad_qkv, grad_out, grad_gate_up, grad_down, grad_gains = pull_back(out_grad.astype(jnp.float32))
    moment_qkv_new, square_qkv_new, update_qkv = adamw_step(qkv_weight, grad_qkv, moment_qkv, square_qkv)
    moment_out_new, square_out_new, update_out = adamw_step(out_weight, grad_out, moment_out, square_out)
    moment_gate_up_new, square_gate_up_new, update_gate_up = adamw_step(gate_up_weight, grad_gate_up, moment_gate_up, square_gate_up)
    moment_down_new, square_down_new, update_down = adamw_step(down_weight, grad_down, moment_down, square_down)
    moment_gains_new, square_gains_new, update_gains = adamw_step(norm_gains, grad_gains, moment_gains, square_gains)
    return (block_val.astype(jnp.bfloat16), input_grad, grad_qkv, grad_out, grad_gate_up, grad_down, grad_gains, moment_qkv_new, moment_out_new, moment_gate_up_new, moment_down_new, moment_gains_new, square_qkv_new, square_out_new, square_gate_up_new, square_down_new, square_gains_new, update_qkv, update_out, update_gate_up, update_down, update_gains)
```

```python
import math

import jax
import jax.numpy as jnp
from jax import lax
from jax.sharding import Mesh, PartitionSpec as P

HEADS = 8
KV = 4
HEAD = 256
MEAN_LEN = 1024


NORM_EPS = 1e-06
SOFT_CAP = 50.0
MASKED_SCORE = -1e30
BETA_ONE = 0.9
BETA_TWO = 0.95
FIRST_FIX = 1.0 - 0.9**10
SECOND_FIX = 1.0 - 0.95**10
LEARN_RATE = 0.05
WEIGHT_DECAY = 0.1
ADAM_EPS = 1e-08


def shifted(block, axis, distance):
    devices = range(lax.axis_size(axis))
    route = [(i - distance, i) for i in devices if i - distance in devices]
    return lax.ppermute(block, axis, route)


def rms_norm(values, gain_row):
    return (
        values
        * lax.rsqrt(jnp.mean(values * values, axis=-1, keepdims=True) + NORM_EPS)
        * (1.0 + gain_row)
    )


def rotate(tensor, cosine, sine_part):
    half_dim = tensor.shape[-1] // 2
    leading = tensor[..., :half_dim]
    trailing = tensor[..., half_dim:]
    return jnp.concatenate(
        [leading * cosine - trailing * sine_part, trailing * cosine + leading * sine_part], axis=-1
    )


def geglu_mix(gate_pre, up_pre):
    return jax.nn.gelu(gate_pre, approximate=True) * up_pre


def adamw_step(weight, gradient, moment, square):
    weight_wide = weight.astype(jnp.float32)
    moment_new = BETA_ONE * moment + (1.0 - BETA_ONE) * gradient
    square_new = BETA_TWO * square + (1.0 - BETA_TWO) * gradient * gradient
    update = -LEARN_RATE * (
        moment_new / FIRST_FIX / (jnp.sqrt(square_new / SECOND_FIX) + ADAM_EPS)
        + WEIGHT_DECAY * weight_wide
    )
    return (moment_new, square_new, update)


def capped_scores(query_rot, key_part, allowed):
    raw_scores = jnp.einsum(
        "qkgd,skd->kgqs", query_rot, key_part, preferred_element_type=jnp.float32
    )
    bent_raw = jnp.tanh(raw_scores / SOFT_CAP)
    return (bent_raw, jnp.where(allowed, SOFT_CAP * bent_raw, MASKED_SCORE))


def split_axes(mesh):
    gx_count, gy_count = mesh.shape["gx"], mesh.shape["gy"]
    fold = 4
    return Mesh(mesh.devices.reshape(gx_count, fold, gy_count // fold), ("gx", "gf", "gt"))


def exchange(blocks, axis):
    count = lax.axis_size(axis)
    mine = lax.axis_index(axis)
    received = blocks
    for step in range(1, count):
        target = (mine + step) % count
        sent = lax.dynamic_index_in_dim(blocks, target, 0, keepdims=True)
        got = lax.ppermute(sent, axis, [(i, (i + step) % count) for i in range(count)])
        received = lax.dynamic_update_slice_in_dim(received, got, (mine - step) % count, 0)
    return received


def collect(block, axis):
    if lax.axis_size(axis) != 2:
        return lax.all_gather(block, axis, axis=1)
    other = lax.ppermute(block, axis, [(0, 1), (1, 0)])
    first = lax.axis_index(axis) == 0
    return jnp.stack([jnp.where(first, block, other), jnp.where(first, other, block)], axis=1)


def reduce_out(blocks, axis):
    if lax.axis_size(axis) != 2:
        return lax.psum_scatter(blocks, axis, scatter_dimension=1, tiled=False)
    mine = lax.axis_index(axis)
    sent = lax.dynamic_index_in_dim(blocks, 1 - mine, 1, keepdims=False)
    kept = lax.dynamic_index_in_dim(blocks, mine, 1, keepdims=False)
    got = lax.ppermute(sent, axis, [(0, 1), (1, 0)])
    return (kept.astype(jnp.float32) + got.astype(jnp.float32)).astype(jnp.bfloat16)


def local(
    hidden_in,
    out_grad,
    seq_ids,
    qkv_weight,
    out_weight,
    gate_up_weight,
    down_weight,
    norm_gains,
    moment_qkv,
    moment_out,
    moment_gate_up,
    moment_down,
    moment_gains,
    square_qkv,
    square_out,
    square_gate_up,
    square_down,
    square_gains,
):
    f32, bf16 = jnp.float32, jnp.bfloat16
    rows_here = hidden_in.shape[0]
    local_kv = qkv_weight.shape[1]
    group_size = HEADS // KV
    gx_count = lax.axis_size("gx")
    fold = lax.axis_size("gf")
    spread = lax.axis_size("gt")
    gy_count = fold * spread
    gy_index = lax.axis_index("gf") * spread + lax.axis_index("gt")
    gx_index = lax.axis_index("gx")
    gy = ("gf", "gt")
    team = ("gx", "gf")
    part = rows_here // gx_count
    feat = hidden_in.shape[1] * gx_count
    depth = gate_up_weight.shape[0]
    ff_here = gate_up_weight.shape[2]
    ff_part = ff_here // fold
    reach_back = min((2 * MEAN_LEN - 2) // rows_here + 1, gy_count - 1)
    whole_keys = gy_count == reach_back + 2 or gy_count == reach_back + 1

    hidden_all = lax.all_gather(hidden_in, "gx", axis=1, tiled=True)
    qkv_all = lax.all_gather(qkv_weight[:, 0], gy, axis=0, tiled=True)
    gains_all = lax.all_gather(norm_gains, gy, axis=1, tiled=True)
    out_all = lax.all_gather(out_weight, gy, axis=1, tiled=True)

    three = jnp.stack([gate_up_weight[:, 0], gate_up_weight[:, 1], down_weight.T], axis=0)
    three = three.reshape(3, depth, fold, ff_part).transpose(2, 0, 1, 3)
    gate_up_got = exchange(three[:, :2], "gf")
    down_got = exchange(three[:, 2], "gf")
    gate_w = collect(gate_up_got[:, 0], "gt").reshape(feat, ff_part)
    up_w = collect(gate_up_got[:, 1], "gt").reshape(feat, ff_part)
    down_w = collect(down_got, "gt").reshape(feat, ff_part)

    gains_wide = gains_all.astype(f32)
    hidden_wide = hidden_all.astype(f32)
    first_row = gy_index * rows_here
    query_index = first_row + jnp.arange(rows_here, dtype=jnp.int32)
    inverse = jnp.exp(jnp.arange(HEAD // 2, dtype=f32) * (-2.0 * math.log(10000.0) / HEAD))
    angles = query_index.astype(f32)[:, None] * inverse[None, :]
    cosine = jnp.cos(angles)
    sine_part = jnp.sin(angles)
    cos_query = cosine[:, None, :]
    sin_query = sine_part[:, None, :]
    query_scale = HEAD ** (-0.5)
    normed_one = rms_norm(hidden_wide, gains_wide[0]).astype(bf16)
    projected = jnp.dot(normed_one, qkv_all, preferred_element_type=f32)
    query_raw = projected[:, : group_size * HEAD].reshape(rows_here, group_size, HEAD)
    key_raw = projected[:, group_size * HEAD : (group_size + 1) * HEAD]
    value_raw = projected[:, (group_size + 1) * HEAD :]
    query_rot = (rotate(query_raw, cos_query, sin_query) * query_scale).astype(bf16)
    key_rot = rotate(key_raw, cosine, sine_part).astype(bf16)
    key_value = jnp.concatenate([key_rot, value_raw.astype(bf16)], axis=-1)
    if whole_keys:
        key_value_all = lax.all_gather(key_value, gy, axis=0, tiled=True)
        key_index = jnp.arange(gy_count * rows_here, dtype=jnp.int32)
        key_seq = seq_ids
    else:
        kv_blocks = [key_value]
        for offset in range(1, reach_back + 1):
            kv_blocks.append(shifted(key_value, gy, offset))
        key_value_all = jnp.concatenate(kv_blocks, axis=0)
        key_index = jnp.concatenate(
            [
                (gy_index - offset) * rows_here + jnp.arange(rows_here, dtype=jnp.int32)
                for offset in range(reach_back + 1)
            ]
        )
        key_seq = jnp.concatenate(
            [
                lax.dynamic_slice_in_dim(
                    seq_ids, jnp.maximum((gy_index - offset) * rows_here, 0), rows_here, 0
                )
                for offset in range(reach_back + 1)
            ]
        )
    query_seq = lax.dynamic_slice_in_dim(seq_ids, first_row, rows_here, 0)
    allowed = (
        (key_index[None, :] >= 0)
        & (key_index[None, :] <= query_index[:, None])
        & (key_seq[None, :] == query_seq[:, None])
    )
    key_part = key_value_all[:, :HEAD]
    value_part = key_value_all[:, HEAD:]
    raw_scores = jnp.einsum("qgd,sd->gqs", query_rot, key_part, preferred_element_type=f32)
    bent_raw = jnp.tanh(raw_scores / SOFT_CAP)
    scores = jnp.where(allowed, SOFT_CAP * bent_raw, MASKED_SCORE)
    row_top = jnp.max(scores, axis=-1, keepdims=True)
    exp_scores = jnp.exp(scores - row_top)
    row_total = jnp.sum(exp_scores, axis=-1, keepdims=True)
    attn_probs = exp_scores / row_total
    probs_low = attn_probs.astype(bf16)
    attended = jnp.einsum("gqs,sd->qgd", probs_low, value_part, preferred_element_type=f32)
    attn_low = attended.astype(bf16).reshape(rows_here, group_size * HEAD)
    mixed_part = jnp.dot(attn_low, out_all, preferred_element_type=f32).astype(bf16)

    def token_sum(partial):
        shared = lax.all_to_all(partial, "gx", 0, 0, tiled=True)
        return jnp.sum(shared.reshape(gx_count, part, feat).astype(f32), axis=0)

    own = lax.dynamic_slice_in_dim(hidden_all, gx_index * part, part, 0).astype(f32)
    grad_own = lax.all_to_all(out_grad, "gx", 0, 1, tiled=True).astype(f32)
    mixed_sum = token_sum(mixed_part)
    branch_one, post_one_back = jax.vjp(rms_norm, mixed_sum, gains_wide[1])
    resid_sum = own + branch_one
    normed_two, norm_two_back = jax.vjp(rms_norm, resid_sum, gains_wide[2])
    normed_all = lax.all_gather(normed_two.astype(bf16), team, axis=0, tiled=True)
    gate_pre = jnp.dot(normed_all, gate_w, preferred_element_type=f32)
    up_pre = jnp.dot(normed_all, up_w, preferred_element_type=f32)
    hidden_act, geglu_back = jax.vjp(geglu_mix, gate_pre, up_pre)
    hidden_act = hidden_act.astype(bf16)
    down_part = jnp.einsum("tf,df->td", hidden_act, down_w, preferred_element_type=f32)
    down_sum = lax.psum_scatter(down_part.astype(bf16), team, scatter_dimension=0, tiled=True)
    down_sum = down_sum.astype(f32)
    branch_two, post_two_back = jax.vjp(rms_norm, down_sum, gains_wide[3])
    block_own = (resid_sum + branch_two).astype(bf16)
    block_out = lax.all_to_all(block_own, "gx", 1, 0, tiled=True)

    down_grad, gain_three = post_two_back(grad_own)
    down_low = lax.all_gather(down_grad.astype(bf16), team, axis=0, tiled=True)
    act_grad = jnp.dot(down_low, down_w, preferred_element_type=f32)
    gate_grad, up_grad = geglu_back(act_grad)
    gate_low, up_low = gate_grad.astype(bf16), up_grad.astype(bf16)
    normed_part = jnp.einsum("tf,df->td", gate_low, gate_w, preferred_element_type=f32)
    normed_part += jnp.einsum("tf,df->td", up_low, up_w, preferred_element_type=f32)
    normed_two_grad = lax.psum_scatter(
        normed_part.astype(bf16), team, scatter_dimension=0, tiled=True
    ).astype(f32)
    three_grad = [
        jnp.einsum("td,tf->df", left, right, preferred_element_type=f32)
        .astype(bf16)
        .reshape(fold, spread, depth, ff_part)
        for left, right in ((normed_all, gate_low), (normed_all, up_low), (down_low, hidden_act))
    ]
    gate_up_sent = jnp.stack([reduce_out(g, "gt") for g in three_grad[:2]], axis=1)
    gate_up_back = exchange(gate_up_sent, "gf").transpose(2, 1, 0, 3)
    grad_gate_up = gate_up_back.reshape(depth, 2, ff_here).astype(f32)
    down_back = exchange(reduce_out(three_grad[2], "gt"), "gf")
    grad_down = down_back.transpose(0, 2, 1).reshape(ff_here, depth).astype(f32)

    resid_part, gain_two = norm_two_back(normed_two_grad)
    resid_grad = grad_own + resid_part
    mixed_grad, gain_one = post_one_back(resid_grad)
    mixed_low = lax.all_gather(mixed_grad.astype(bf16), "gx", axis=0, tiled=True)
    attn_grad = jnp.einsum("td,cd->tc", mixed_low, out_all, preferred_element_type=f32)
    attn_grad = attn_grad.astype(bf16).reshape(rows_here, group_size, HEAD)
    out_weight_grad = jnp.einsum("tc,td->cd", attn_low, mixed_low, preferred_element_type=f32)
    prob_grad = jnp.einsum("qgd,sd->gqs", attn_grad, value_part, preferred_element_type=f32)
    row_delta = jnp.sum(attn_probs * prob_grad, axis=-1, keepdims=True)
    raw_grad = (attn_probs * (prob_grad - row_delta) * (1.0 - bent_raw * bent_raw)).astype(bf16)
    query_grad = jnp.einsum("gqs,sd->qgd", raw_grad, key_part, preferred_element_type=f32)
    key_value_grad = jnp.concatenate(
        [
            jnp.einsum("gqs,qgd->sd", raw_grad, query_rot, preferred_element_type=f32),
            jnp.einsum("gqs,qgd->sd", probs_low, attn_grad, preferred_element_type=f32),
        ],
        axis=-1,
    )
    if whole_keys:
        kv_grad_mine = lax.psum_scatter(
            key_value_grad.astype(bf16), gy, scatter_dimension=0, tiled=True
        ).astype(f32)
    else:
        kv_grad_mine = key_value_grad[:rows_here]
        for offset in range(1, reach_back + 1):
            kv_grad_mine = kv_grad_mine + shifted(
                key_value_grad[offset * rows_here : (offset + 1) * rows_here].astype(bf16),
                gy,
                -offset,
            ).astype(f32)
    key_grad = rotate(kv_grad_mine[:, :HEAD], cosine, -sine_part)
    value_grad = kv_grad_mine[:, HEAD:]
    query_raw_grad = rotate(query_grad * query_scale, cos_query, -sin_query).reshape(
        rows_here, group_size * HEAD
    )
    projected_low = jnp.concatenate([query_raw_grad, key_grad, value_grad], axis=-1).astype(bf16)
    qkv_weight_grad = jnp.einsum("td,tc->dc", normed_one, projected_low, preferred_element_type=f32)
    normed_one_part = jnp.einsum("tc,dc->td", projected_low, qkv_all, preferred_element_type=f32)
    normed_one_grad = token_sum(normed_one_part.astype(bf16))
    _, norm_one_back = jax.vjp(rms_norm, own, gains_wide[0])
    hidden_part, gain_zero = norm_one_back(normed_one_grad)
    input_grad = lax.all_to_all(resid_grad + hidden_part, "gx", 1, 0, tiled=True)
    gains_grad = jnp.stack([gain_zero, gain_one, gain_two, gain_three], axis=0)
    grad_qkv = lax.psum_scatter(
        qkv_weight_grad.astype(bf16), gy, scatter_dimension=0, tiled=True
    ).astype(f32)[:, None]
    grad_out = lax.psum_scatter(
        out_weight_grad.astype(bf16), gy, scatter_dimension=1, tiled=True
    ).astype(f32)
    gains_sum = lax.psum(gains_grad, ("gx", "gf", "gt"))
    grad_gains = lax.dynamic_slice_in_dim(gains_sum, gy_index * depth, depth, 1)

    moment_qkv_new, square_qkv_new, update_qkv = adamw_step(
        qkv_weight, grad_qkv, moment_qkv, square_qkv
    )
    moment_out_new, square_out_new, update_out = adamw_step(
        out_weight, grad_out, moment_out, square_out
    )
    moment_gate_up_new, square_gate_up_new, update_gate_up = adamw_step(
        gate_up_weight, grad_gate_up, moment_gate_up, square_gate_up
    )
    moment_down_new, square_down_new, update_down = adamw_step(
        down_weight, grad_down, moment_down, square_down
    )
    moment_gains_new, square_gains_new, update_gains = adamw_step(
        norm_gains, grad_gains, moment_gains, square_gains
    )
    return (
        block_out,
        input_grad,
        grad_qkv,
        grad_out,
        grad_gate_up,
        grad_down,
        grad_gains,
        moment_qkv_new,
        moment_out_new,
        moment_gate_up_new,
        moment_down_new,
        moment_gains_new,
        square_qkv_new,
        square_out_new,
        square_gate_up_new,
        square_down_new,
        square_gains_new,
        update_qkv,
        update_out,
        update_gate_up,
        update_down,
        update_gains,
    )


def solution(mesh):
    return jax.shard_map(
        local,
        mesh=split_axes(mesh),
        in_specs=(
            P(("gf", "gt"), "gx"),
            P(("gf", "gt"), "gx"),
            P(),
            P(("gf", "gt"), "gx", None),
            P("gx", ("gf", "gt")),
            P(("gf", "gt"), None, "gx"),
            P("gx", ("gf", "gt")),
            P(None, ("gf", "gt")),
            P(("gf", "gt"), "gx", None),
            P("gx", ("gf", "gt")),
            P(("gf", "gt"), None, "gx"),
            P("gx", ("gf", "gt")),
            P(None, ("gf", "gt")),
            P(("gf", "gt"), "gx", None),
            P("gx", ("gf", "gt")),
            P(("gf", "gt"), None, "gx"),
            P("gx", ("gf", "gt")),
            P(None, ("gf", "gt")),
        ),
        out_specs=(
            P(("gf", "gt"), "gx"),
            P(("gf", "gt"), "gx"),
            P(("gf", "gt"), "gx", None),
            P("gx", ("gf", "gt")),
            P(("gf", "gt"), None, "gx"),
            P("gx", ("gf", "gt")),
            P(None, ("gf", "gt")),
            P(("gf", "gt"), "gx", None),
            P("gx", ("gf", "gt")),
            P(("gf", "gt"), None, "gx"),
            P("gx", ("gf", "gt")),
            P(None, ("gf", "gt")),
            P(("gf", "gt"), "gx", None),
            P("gx", ("gf", "gt")),
            P(("gf", "gt"), None, "gx"),
            P("gx", ("gf", "gt")),
            P(None, ("gf", "gt")),
            P(("gf", "gt"), "gx", None),
            P("gx", ("gf", "gt")),
            P(("gf", "gt"), None, "gx"),
            P("gx", ("gf", "gt")),
            P(None, ("gf", "gt")),
        ),
        check_vma=False,
    )
```
